512 devices in a mesh: dp: 16 (over y, core), expert: 8 (over z), tensor: 4 (over x).
Axes of the slice: x: 4, y: 8, z: 8, core: 2. Of those that a mesh axis runs over, the one named last changes fastest.
Arguments:
- tokens: bfloat16 [8192, 4096], P(('dp', 'expert'), 'tensor'), may hold values from -6 to 6
- expert_ids: int32 [8192, 8], P(('dp', 'expert')), may hold values from 0 to 127, all different within a row; in each aligned block of 64 rows (0 to 63, 64 to 127, ...) at most 6 rows name the same one
- combine_weights: float32 [8192, 8], P(('dp', 'expert')), may hold values from 0.05 to 1
- topology: int32 [128, 12, 12], P(('dp', 'expert'), 'tensor'), may hold values from 0 to 31, all different within a row
- gate_blocks: bfloat16 [128, 12, 12, 128, 128], P(('dp', 'expert'), 'tensor'), may hold values from -0.15625 to 0.15625
- up_blocks: bfloat16 [128, 12, 12, 128, 128], P(('dp', 'expert'), 'tensor'), may hold values from -0.15625 to 0.15625
- down_blocks: bfloat16 [128, 12, 12, 128, 128], P(('dp', 'expert'), 'tensor'), may hold values from -0.25 to 0.25
Outputs:
- layer_out: bfloat16 [8192, 4096], P(('dp', 'expert'), 'tensor')
The draws below stay inside these ranges and needn't reach their ends.
Inputs may be any that keep to these rules, and one draw needn't show every extreme that they name: `expert_ids`: in each aligned block of 64 tokens (the tokens of one index of dp+expert), no expert is named more than 6 times, a bound that some block reaches; a token names 8 different experts. `topology`: each row names 12 different blocks; every block is named by some row.
All inputs are finite; a program needn't handle non-finite values.
Results may differ from the reference program's by a relative error of at most 0.0058.
Values may be sent and summed in bfloat16 or wider, within the bound.
A program may use at most 128 MiB of HBM per device.

```python
import math
import jax
import jax.numpy as jnp
import numpy as np
from jax import lax

D = 4096
FF = 1536
TOP = 8
BLK = 128
KB = 12
TOK_DEV = 64
EXPERTS = 128
CAP = 6
TOKENS = 8192
N_TENSOR = 4


def levels(own_key, shape, shards, least, high):
    level, own = 1.0, jax.random.fold_in(own_key, 6)
    for axis_at, parts in shards:
        draws = jnp.exp(jax.random.uniform(jax.random.fold_in(own, axis_at), (parts,), jnp.float32, least / len(shards), high / len(shards)))
        level = level * jnp.repeat(draws, shape[axis_at] // parts).reshape([-1 if axis == axis_at else 1 for axis in range(len(shape))])
    return level


def different_ones(stream_key, rows, amount, top, lift):
    order = jax.random.permutation(jax.random.fold_in(stream_key, 1), amount)
    favour = order
    for power in range(3):
        favour = favour * favour // amount
    favour = favour * lift // amount
    tickets = jax.random.randint(jax.random.fold_in(stream_key, 2), (rows, amount), 0, 4096) + favour
    holders = jax.random.permutation(jax.random.fold_in(stream_key, 3), rows)[jnp.arange(amount) % rows]
    tickets = jnp.where(jnp.arange(rows)[:, None] == holders[None, :], 1 << 14, tickets)
    merit = tickets * amount + jnp.arange(amount)
    return lax.top_k(merit.astype(jnp.int32), top)[1].astype(jnp.int32)


def shared_out(own_key, own, number, rows, number_of, top, reach, slope):
    sequence = jax.random.permutation(own_key, number_of)
    heavy_load, common = portions_of(number_of, rows * top, reach, slope, True), portions_of(number_of, rows * top, reach, slope, False)
    places = jnp.arange(number_of)

    def named(tallies, rotation):
        used = int((tallies > 0).sum())
        fixed = max(1, used // 4)
        shifted = fixed + (places - fixed + rotation * (used - fixed)) % max(1, number_of - fixed)
        return jnp.zeros((number_of,), jnp.int32).at[sequence[jnp.where(places < fixed, places, shifted)]].set(jnp.asarray(tallies, jnp.int32))

    tallies = jnp.where(number % 4 == 0, named(heavy_load, number // 4), named(common, number - number // 4 - 1))
    mixed = jax.random.permutation(jax.random.fold_in(own, 3), number_of)
    source_of, receiver = mixed[0:number_of // 2 * 2:2], mixed[1:number_of // 2 * 2:2]
    room = jnp.minimum(tallies[source_of] - 1, reach - tallies[receiver]) // 2
    room = jnp.where((source_of == sequence[0]) | (receiver == sequence[0]) | (tallies[receiver] == 0), 0, jnp.maximum(room, 0))
    shifted = jax.random.randint(jax.random.fold_in(own, 4), (number_of // 2,), 0, 1 << 20) % (room + 1)
    tallies = tallies.at[source_of].add(-shifted).at[receiver].add(shifted)
    items = jnp.searchsorted(jnp.cumsum(tallies), jnp.arange(rows * top), side="right").astype(jnp.int32)
    listing = items.reshape(top, rows).T
    listing = listing[jax.random.permutation(jax.random.fold_in(own, 1), rows)]
    rotation = jax.random.randint(jax.random.fold_in(own, 2), (rows, 1), 0, top)
    return jnp.take_along_axis(listing, (jnp.arange(top)[None, :] + rotation) % top, axis=1)


def portions_of(number_of, total, limit, slope, full):
    loads = [(1 << 20) // math.isqrt(rank ** slope) + 1 for rank in range(1, number_of + 1)]
    largest = limit if full else min(limit, max(-(-total // number_of), total * loads[0] // sum(loads)))
    least = 1 if total - largest >= number_of - 1 else 0
    holding, spare = [largest] + [least] * (number_of - 1), total - largest - least * (number_of - 1)
    while spare > 0:
        candidates = [i for i in range(1, number_of) if holding[i] < largest] or [i for i in range(1, number_of) if holding[i] < limit]
        pool, remaining = sum([loads[i] for i in candidates]), spare
        for i in candidates:
            more = min(limit - holding[i], max(1, remaining * loads[i] // pool), spare)
            holding[i] = holding[i] + more
            spare = spare - more
    return np.array(holding)


def noise(key, extent, deviation, reach, shards=(), kind=jnp.bfloat16):
    gain = levels(key, extent, shards, -0.22, 0.18) if shards else 1.0
    values = jax.random.normal(key, extent, jnp.float32) * deviation * gain
    return jnp.minimum(jnp.maximum(values, -reach), reach).astype(kind)


def setup_inputs(seed: int = 0) -> dict:
    key_list = jax.random.split(jax.random.key(seed), 8)
    tokens = noise(key_list[0], (TOKENS, D), 1.0, 6.0, ((0, 128), (1, 4)))
    expert_ids_keys = jax.random.split(jax.random.fold_in(key_list[1], 1), TOKENS // TOK_DEV)
    expert_ids_turns = jax.random.permutation(jax.random.fold_in(key_list[1], 3), TOKENS // TOK_DEV)
    expert_ids = jax.vmap(lambda own, number: shared_out(jax.random.fold_in(key_list[1], 2), own, number, TOK_DEV, EXPERTS, TOP, CAP, 2))(expert_ids_keys, expert_ids_turns).reshape((TOKENS, TOP))
    combine_weights = jnp.clip(0.05 + 0.95 * jax.random.uniform(key_list[2], (TOKENS, TOP), jnp.float32) ** levels(key_list[2], (TOKENS, TOP), ((0, 128),), -0.2, 0.2), 0.05, 1.0)
    topology = different_ones(key_list[3], EXPERTS * (FF // BLK), D // BLK, KB, 0).reshape((EXPERTS, FF // BLK, KB))
    gate_blocks = noise(key_list[4], (EXPERTS, FF // BLK, KB, BLK, BLK), (KB * BLK) ** -0.5, 0.15625, ((0, 128), (1, 4)))
    up_blocks = noise(key_list[5], (EXPERTS, FF // BLK, KB, BLK, BLK), (KB * BLK) ** -0.5, 0.15625, ((0, 128), (1, 4)))
    down_blocks = noise(key_list[6], (EXPERTS, FF // BLK, KB, BLK, BLK), (FF * KB * BLK // D) ** -0.5, 0.25, ((0, 128), (1, 4)))
    return dict(tokens=tokens, expert_ids=expert_ids, combine_weights=combine_weights, topology=topology, gate_blocks=gate_blocks, up_blocks=up_blocks, down_blocks=down_blocks)


def slot_numbers(expert_ids):
    groups = expert_ids.shape[0] // TOK_DEV
    picked_ids = expert_ids.reshape(groups, TOK_DEV * TOP)
    onehot = (picked_ids[:, :, None] == jnp.arange(EXPERTS, dtype=jnp.int32)[None, None, :]).astype(jnp.int32)
    before = jnp.cumsum(onehot, axis=1) - onehot
    return jnp.sum(before * onehot, axis=2).reshape(expert_ids.shape).astype(jnp.int32)


def expert_rows(rows, layout_ids, gate_part, up_part, down_part):
    row_count = rows.shape[0]
    blocked = rows.reshape(row_count, D // BLK, BLK).astype(jnp.float32)
    local_blocks = FF // BLK // N_TENSOR
    placer = (layout_ids[:, :, None] == jnp.arange(D // BLK, dtype=jnp.int32)[None, None, :]).astype(jnp.float32)
    total_out = jnp.zeros((row_count, D // BLK, BLK), jnp.float32)
    for quarter in range(N_TENSOR):
        start_block = quarter * local_blocks
        end_block = start_block + local_blocks
        chosen = layout_ids[start_block:end_block].reshape(-1).astype(jnp.int32)
        picked = jnp.take(blocked, chosen, axis=1).reshape(row_count, local_blocks, KB, BLK)
        gate_proj = jnp.einsum('rhkc,hkcf->rhf', picked, gate_part[start_block:end_block].astype(jnp.float32))
        up_proj = jnp.einsum('rhkc,hkcf->rhf', picked, up_part[start_block:end_block].astype(jnp.float32))
        hidden = (jax.nn.silu(gate_proj) * up_proj).astype(jnp.bfloat16)
        pieces = jnp.einsum('rhf,hkfc->rhkc', hidden.astype(jnp.float32), down_part[start_block:end_block].astype(jnp.float32))
        partial_value = jnp.einsum('rhkc,hkb->rbc', pieces, placer[start_block:end_block], precision=lax.Precision.HIGHEST)
        rounded = lax.optimization_barrier(partial_value.astype(jnp.bfloat16))
        total_out = total_out + rounded.astype(jnp.float32)
    return total_out.reshape(row_count, D)


def reference(tokens, expert_ids, combine_weights, topology, gate_blocks, up_blocks, down_blocks):
    groups = TOKENS // TOK_DEV
    slot_index = slot_numbers(expert_ids)
    owner_group = (jnp.arange(TOKENS, dtype=jnp.int32) // TOK_DEV).astype(jnp.int32)
    positions = (owner_group[:, None] * CAP + slot_index).astype(jnp.int32)
    token_index = jnp.broadcast_to(jnp.arange(TOKENS, dtype=jnp.int32)[:, None], (TOKENS, TOP))
    slot_table = jnp.full((EXPERTS, groups * CAP), TOKENS, jnp.int32)
    slot_table = slot_table.at[expert_ids.reshape(-1), positions.reshape(-1)].set(token_index.reshape(-1))
    weight_table = jnp.zeros((EXPERTS, groups * CAP), jnp.float32)
    weight_table = weight_table.at[expert_ids.reshape(-1), positions.reshape(-1)].set(combine_weights.reshape(-1))
    padded = jnp.concatenate([tokens, jnp.zeros((1, D), jnp.bfloat16)], axis=0)

    def per_expert(running, scanned):
        row_index, weights, layout_ids, gate_part, up_part, down_part = scanned
        results = expert_rows(padded[row_index], layout_ids, gate_part, up_part, down_part)
        return running.at[row_index].add(weights[:, None] * results), None

    initial = jnp.zeros((TOKENS + 1, D), jnp.float32)
    summed_out, _ = lax.scan(per_expert, initial, (slot_table, weight_table, topology, gate_blocks, up_blocks, down_blocks))
    return summed_out[:TOKENS].astype(jnp.bfloat16)
```

```python
import functools

import jax
import jax.numpy as jnp
from jax import lax
from jax.experimental import pallas as pl
from jax.experimental.pallas import tpu as pltpu
from jax.sharding import PartitionSpec as P

BLK = 128
PIECES = 4
F32, BF16 = jnp.float32, jnp.bfloat16
MESH = pl.DeviceIdType.MESH


def matmul(a, b):
    return jnp.dot(a, b, preferred_element_type=F32)


def layer_kernel(cfg, tok, ids, wts, inv, gate, up, down, out, *scratch):
    n_dp, n_z, n_x, cap, toks, width, kb, hb = cfg
    (gbuf, ubuf, dbuf, gu, dn, tabs_out, tabs, tokp, zbuf, qa, va, disp, ct, comb_hi, comb_lo, ysend, xin, acc, hid,
     asend, arecv, bsend_r, bsend_l, brecv_l, brecv_r, fsend, yret, gsend, zret,
     w_sem, t_send, t_recv, z_send, z_recv, y_send, y_recv, r1_send, l1_send, r1_recv, l1_recv, r2_send, l2_send,
     r2_recv, l2_recv, ar_send, al_send, ar_recv, al_recv, br_send, bl_send, br_recv, bl_recv,
     f_send, f_recv, g_send, g_recv) = scratch
    pieces = xin.shape[1]
    w = width // pieces
    grp = n_z * cap
    rows = n_dp * grp
    half = rows // 2
    all_tok = n_z * toks
    hid_w = hb * BLK
    per = w // BLK
    dp, z, x = lax.axis_index("dp"), lax.axis_index("expert"), lax.axis_index("tensor")
    right, left, far = lax.rem(x + 1, n_x), lax.rem(x + n_x - 1, n_x), lax.rem(x + 2, n_x)

    def remote(src, dst, ssem, rsem, where):
        return pltpu.make_async_remote_copy(
            src_ref=src, dst_ref=dst, send_sem=ssem, recv_sem=rsem, device_id=where, device_id_type=MESH)

    def drain(ref, sem):
        pltpu.make_async_copy(ref, ref, sem).wait()

    weight_copies = [
        pltpu.make_async_copy(src.at[0], buf.at[:, pl.ds(0, kb)], w_sem.at[i])
        for i, (src, buf) in enumerate(((gate, gbuf), (up, ubuf), (down, dbuf)))
    ]
    for c in weight_copies:
        c.start()

    barrier = pltpu.get_barrier_semaphore()

    def greet_dp(i, _):
        pl.semaphore_signal(barrier, inc=1, device_id={"dp": lax.rem(dp + i, n_dp)}, device_id_type=MESH)
        return 0

    def greet_z(i, _):
        pl.semaphore_signal(barrier, inc=1, device_id={"expert": lax.rem(z + i, n_z)}, device_id_type=MESH)
        return 0

    lax.fori_loop(1, n_dp, greet_dp, 0)
    lax.fori_loop(1, n_z, greet_z, 0)
    pl.semaphore_signal(barrier, inc=1, device_id={"tensor": right}, device_id_type=MESH)
    pl.semaphore_signal(barrier, inc=1, device_id={"tensor": left}, device_id_type=MESH)

    n_e = n_z * n_dp
    q = lax.broadcasted_iota(jnp.int32, (n_e, 2 * toks), 0)
    lane = lax.broadcasted_iota(jnp.int32, (n_e, 2 * toks), 1)
    shift = n_dp.bit_length() - 1
    expert = (q & (n_dp - 1)) * n_z + (q >> shift)
    named = jnp.zeros((n_e, 2 * toks), F32)
    weight = jnp.zeros((n_e, 2 * toks), F32)
    for k in range(ids.shape[0]):
        same = ids[k : k + 1, :] == expert
        named = named + jnp.where(same, 1.0, 0.0)
        weight = weight + jnp.where(same, wts[k : k + 1, :], 0.0)
    before = lax.broadcasted_iota(jnp.int32, (2 * toks, 2 * toks), 0)
    after = lax.broadcasted_iota(jnp.int32, (2 * toks, 2 * toks), 1) & (toks - 1)
    earlier = jnp.where((before < after) & (before < toks), 1.0, 0.0).astype(BF16)
    slot = matmul(named.astype(BF16), earlier)
    table = jnp.where(lane < toks, jnp.where(named > 0.5, slot, -1.0), weight)
    tabs_out[...] = table.reshape(n_z, n_dp, 2 * toks)
    for p in range(pieces):
        tokp[p] = tok[:, p * w : (p + 1) * w]

    pl.semaphore_wait(barrier, (n_dp - 1) + (n_z - 1) + 2)

    def send_table(i, _):
        to = lax.rem(z + i, n_z)
        remote(tabs_out.at[to], tabs.at[z], t_send, t_recv, {"expert": to}).start()
        return 0

    lax.fori_loop(1, n_z, send_table, 0)

    def send_tokens(j, _):
        p, i = j // (n_z - 1), lax.rem(j, n_z - 1) + 1
        remote(tokp.at[p], zbuf.at[p, z], z_send.at[p], z_recv.at[p], {"expert": lax.rem(z + i, n_z)}).start()
        return 0

    lax.fori_loop(0, pieces * (n_z - 1), send_tokens, 0)
    tabs[z] = tabs_out[z]
    for p in range(pieces):
        zbuf[p, z] = tokp[p]

    for buf in (gbuf, ubuf, dbuf):
        buf[:, kb] = jnp.zeros((hb, BLK, BLK), BF16)
    acc[...] = jnp.zeros(acc.shape, F32)
    for c in weight_copies:
        c.wait()

    def dense(i, _):
        for j in range(per):
            b = i * per + j
            for h in range(hb):
                at = inv[h, b]
                gu[i, j * BLK : (j + 1) * BLK, h * BLK : (h + 1) * BLK] = gbuf[h, at]
                gu[i, j * BLK : (j + 1) * BLK, hid_w + h * BLK : hid_w + (h + 1) * BLK] = ubuf[h, at]
                dn[i, h * BLK : (h + 1) * BLK, j * BLK : (j + 1) * BLK] = dbuf[h, at]
        return 0

    lax.fori_loop(0, n_x * pieces, dense, 0)

    drain(tabs.at[pl.ds(0, n_z - 1)], t_recv)
    low = lax.broadcasted_iota(jnp.int32, (n_dp, 2 * toks), 1) < toks
    for j in range(n_z // 2):
        one, two = tabs[2 * j], tabs[2 * j + 1]
        qa[:, j * 2 * toks : (j + 1) * 2 * toks] = jnp.where(low, one, pltpu.roll(two, toks, 1))
        va[:, j * 2 * toks : (j + 1) * 2 * toks] = jnp.where(low, pltpu.roll(one, toks, 1), two)
    r = lax.broadcasted_iota(jnp.int32, (grp, all_tok), 0)
    home = jnp.zeros((grp, all_tok), jnp.int32)
    for j in range(1, n_z):
        home = home + jnp.where(r >= cap * j, 1, 0)
    home_of_token = lax.broadcasted_iota(jnp.int32, (grp, all_tok), 1) >> (toks.bit_length() - 1)
    wanted = jnp.where(home == home_of_token, r - cap * home, -2).astype(F32)

    def one_hot(d, _):
        hit = jnp.broadcast_to(qa[pl.ds(d, 1), :], (grp, all_tok)) == wanted
        at = pl.ds(pl.multiple_of(d * grp, grp), grp)
        disp[at, :] = jnp.where(hit, 1.0, 0.0).astype(BF16)
        ct[at, :] = jnp.where(hit, jnp.broadcast_to(va[pl.ds(d, 1), :], (grp, all_tok)), 0.0)
        return 0

    lax.fori_loop(0, n_dp, one_hot, 0)

    third = rows // 3

    def gather_piece(p):
        drain(zbuf.at[p, pl.ds(0, n_z - 1)], z_recv.at[p])
        t = zbuf[p].reshape(all_tok, w)

        def tile(i, _):
            at = pl.ds(pl.multiple_of(i * third, 16), third)
            ysend[p, at, :] = matmul(disp[at, :], t).astype(BF16)
            return 0

        lax.fori_loop(0, 3, tile, 0)
        mine = pl.ds(pl.multiple_of(dp * grp, 16), grp)

        def send(i, _):
            to = lax.rem(dp + i, n_dp)
            remote(ysend.at[p, pl.ds(pl.multiple_of(to * grp, 16), grp)], xin.at[x, p, mine],
                   y_send.at[p], y_recv.at[p], {"dp": to}).start()
            return 0

        lax.fori_loop(1, n_dp, send, 0)
        xin[x, p, mine, :] = ysend[p, mine, :]

    def spread_piece(p):
        drain(xin.at[x, p, pl.ds(0, rows - grp)], y_recv.at[p])
        src = xin.at[x, p]
        remote(src, src, r1_send.at[p], r1_recv.at[p], {"tensor": right}).start()
        remote(src, src, l1_send.at[p], l1_recv.at[p], {"tensor": left}).start()

    def forward_piece(p):
        drain(xin.at[left, p], r1_recv.at[p])
        src = xin.at[left, p, pl.ds(0, half)]
        remote(src, src, r2_send.at[p], r2_recv.at[p], {"tensor": right}).start()
        drain(xin.at[right, p], l1_recv.at[p])
        src = xin.at[right, p, pl.ds(half, half)]
        remote(src, src, l2_send.at[p], l2_recv.at[p], {"tensor": left}).start()

    def add_piece(quarter, p):
        def tile(i, _):
            at = pl.ds(pl.multiple_of(i * third, 16), third)
            acc[at, :] += matmul(xin[quarter, p, at, :], gu[quarter * pieces + p])
            return 0

        lax.fori_loop(0, 3, tile, 0)

    def inward(t, _):
        @pl.when(t < pieces)
        def _():
            gather_piece(t)

        @pl.when((t >= 1) & (t < pieces + 1))
        def _():
            spread_piece(t - 1)

        @pl.when((t >= 2) & (t < pieces + 2))
        def _():
            forward_piece(t - 2)
            add_piece(x, t - 2)
            add_piece(left, t - 2)
            add_piece(right, t - 2)

        @pl.when(t >= 3)
        def _():
            drain(xin.at[far, t - 3, pl.ds(0, half)], r2_recv.at[t - 3])
            drain(xin.at[far, t - 3, pl.ds(half, half)], l2_recv.at[t - 3])
            add_piece(far, t - 3)

        return 0

    tr = min(rows, BLK)
    for j in range(rows // tr):
        c = ct[j * tr : (j + 1) * tr, :].T
        hi = c.astype(BF16)
        comb_hi[:, j * tr : (j + 1) * tr] = hi
        comb_lo[:, j * tr : (j + 1) * tr] = (c - hi.astype(F32)).astype(BF16)

    lax.fori_loop(0, pieces + 3, inward, 0)

    def activate(i, _):
        at = pl.ds(pl.multiple_of(i * third, 16), third)
        g = acc[at, :hid_w]
        hid[at, :] = (g / (1.0 + jnp.exp(-g)) * acc[at, hid_w:]).astype(BF16)
        return 0

    lax.fori_loop(0, 3, activate, 0)

    def partial(quarter, p, part):
        return matmul(hid[part * half : (part + 1) * half, :], dn[quarter * pieces + p])

    lo, hi_ = pl.ds(0, half), pl.ds(half, half)

    def send_far(p):
        asend[p, lo, :] = partial(far, p, 0).astype(BF16)
        remote(asend.at[p, lo], arecv.at[p, lo], ar_send.at[p], ar_recv.at[p], {"tensor": right}).start()
        asend[p, hi_, :] = partial(far, p, 1).astype(BF16)
        remote(asend.at[p, hi_], arecv.at[p, hi_], al_send.at[p], al_recv.at[p], {"tensor": left}).start()

    def send_near(p):
        bsend_r[p, hi_, :] = partial(right, p, 1).astype(BF16)
        bsend_l[p, lo, :] = partial(left, p, 0).astype(BF16)
        drain(arecv.at[p, lo], ar_recv.at[p])
        bsend_r[p, lo, :] = (partial(right, p, 0) + arecv[p, lo, :].astype(F32)).astype(BF16)
        remote(bsend_r.at[p], brecv_l.at[p], br_send.at[p], br_recv.at[p], {"tensor": right}).start()
        drain(arecv.at[p, hi_], al_recv.at[p])
        bsend_l[p, hi_, :] = (partial(left, p, 1) + arecv[p, hi_, :].astype(F32)).astype(BF16)
        remote(bsend_l.at[p], brecv_r.at[p], bl_send.at[p], bl_recv.at[p], {"tensor": left}).start()

    def send_home(p):
        drain(brecv_l.at[p], br_recv.at[p])
        drain(brecv_r.at[p], bl_recv.at[p])
        for part, at in ((0, lo), (1, hi_)):
            total = partial(x, p, part) + brecv_l[p, at, :].astype(F32) + brecv_r[p, at, :].astype(F32)
            fsend[p, at, :] = total.astype(BF16)
        mine = pl.ds(pl.multiple_of(dp * grp, 16), grp)

        def send(i, _):
            to = lax.rem(dp + i, n_dp)
            remote(fsend.at[p, pl.ds(pl.multiple_of(to * grp, 16), grp)], yret.at[p, mine],
                   f_send.at[p], f_recv.at[p], {"dp": to}).start()
            return 0

        lax.fori_loop(1, n_dp, send, 0)
        yret[p, mine, :] = fsend[p, mine, :]

    def combine(p):
        drain(yret.at[p, pl.ds(0, rows - grp)], f_recv.at[p])

        def tile(i, _):
            at = pl.ds(pl.multiple_of(i * 2 * toks, 2 * toks), 2 * toks)
            s = matmul(comb_hi[at, :], yret[p]) + matmul(comb_lo[at, :], yret[p])
            gsend[p, pl.ds(2 * i, 2)] = s.astype(BF16).reshape(2, toks, w)
            return 0

        lax.fori_loop(0, n_z // 2, tile, 0)

        def send(i, _):
            to = lax.rem(z + i, n_z)
            remote(gsend.at[p, to], zret.at[p, z], g_send.at[p], g_recv.at[p], {"expert": to}).start()
            return 0

        lax.fori_loop(1, n_z, send, 0)
        zret[p, z] = gsend[p, z]

    def finish(p):
        drain(zret.at[p, pl.ds(0, n_z - 1)], g_recv.at[p])
        total = zret[p, 0].astype(F32)
        for h in range(1, n_z):
            total = total + zret[p, h].astype(F32)
        out[:, pl.ds(pl.multiple_of(p * w, BLK), w)] = total.astype(BF16)

    send_far(0)
    send_far(1)

    def outward(t, _):
        @pl.when(t < pieces)
        def _():
            send_near(t)

        @pl.when(t + 2 < pieces)
        def _():
            send_far(t + 2)

        @pl.when((t >= 1) & (t < pieces + 1))
        def _():
            send_home(t - 1)

        @pl.when((t >= 2) & (t < pieces + 2))
        def _():
            combine(t - 2)

        @pl.when(t >= 3)
        def _():
            finish(t - 3)

        return 0

    lax.fori_loop(0, pieces + 3, outward, 0)

    drain(tabs_out.at[pl.ds(0, n_z - 1)], t_send)

    def settle(p, _):
        drain(zbuf.at[p, pl.ds(0, n_z - 1)], z_send.at[p])
        drain(ysend.at[p, pl.ds(0, rows - grp)], y_send.at[p])
        drain(xin.at[0, p], r1_send.at[p])
        drain(xin.at[0, p], l1_send.at[p])
        drain(xin.at[0, p, lo], r2_send.at[p])
        drain(xin.at[0, p, lo], l2_send.at[p])
        drain(asend.at[p, lo], ar_send.at[p])
        drain(asend.at[p, lo], al_send.at[p])
        drain(bsend_r.at[p], br_send.at[p])
        drain(bsend_l.at[p], bl_send.at[p])
        drain(fsend.at[p, pl.ds(0, rows - grp)], f_send.at[p])
        drain(gsend.at[p, pl.ds(0, n_z - 1)], g_send.at[p])
        return 0

    lax.fori_loop(0, pieces, settle, 0)


def per_device(tokens, expert_ids, combine_weights, topology, gate_blocks, up_blocks, down_blocks):
    n_dp, n_z, n_x = (lax.axis_size(a) for a in ("dp", "expert", "tensor"))
    toks, width = tokens.shape
    top = expert_ids.shape[1]
    cap = min(toks, 3 * toks * top // (2 * n_dp * n_z))
    _, hb, kb = topology.shape
    n_b = n_x * width // BLK
    pieces, w = PIECES, width // PIECES
    rows, grp = n_dp * n_z * cap, n_z * cap
    ids = jnp.concatenate([expert_ids.T, expert_ids.T], axis=1)
    wts = jnp.concatenate([combine_weights.T, combine_weights.T], axis=1)
    hits = topology[0][:, :, None] == jnp.arange(n_b, dtype=jnp.int32)[None, None, :]
    inv = kb + jnp.sum(jnp.where(hits, jnp.arange(kb, dtype=jnp.int32)[None, :, None] - kb, 0), axis=1)
    vm, dma = pltpu.VMEM, pltpu.SemaphoreType.DMA
    hid_w = hb * BLK
    scratch = (
        [vm((hb, kb + 1, BLK, BLK), BF16)] * 3
        + [
            vm((n_x * pieces, w, 2 * hid_w), BF16),
            vm((n_x * pieces, hid_w, w), BF16),
            vm((n_z, n_dp, 2 * toks), F32),
            vm((n_z, n_dp, 2 * toks), F32),
            vm((pieces, toks, w), BF16),
            vm((pieces, n_z, toks, w), BF16),
            vm((n_dp, n_z * toks), F32),
            vm((n_dp, n_z * toks), F32),
            vm((rows, n_z * toks), BF16),
            vm((rows, n_z * toks), F32),
            vm((n_z * toks, rows), BF16),
            vm((n_z * toks, rows), BF16),
            vm((pieces, rows, w), BF16),
            vm((n_x, pieces, rows, w), BF16),
            vm((rows, 2 * hid_w), F32),
            vm((rows, hid_w), BF16),
        ]
        + [vm((pieces, rows, w), BF16)] * 8
        + [vm((pieces, n_z, toks, w), BF16)] * 2
        + [dma((3,)), dma(()), dma(())]
        + [dma((pieces,))] * 24
    )
    any_ = pl.BlockSpec(memory_space=pl.ANY)
    vmem = pl.BlockSpec(memory_space=pltpu.VMEM)
    return pl.pallas_call(
        functools.partial(layer_kernel, (n_dp, n_z, n_x, cap, toks, width, kb, hb)),
        out_shape=jax.ShapeDtypeStruct((toks, width), BF16),
        in_specs=[vmem, vmem, vmem, pl.BlockSpec(memory_space=pltpu.SMEM), any_, any_, any_],
        out_specs=vmem,
        scratch_shapes=scratch,
        compiler_params=pltpu.CompilerParams(
            collective_id=0, has_side_effects=True, vmem_limit_bytes=60 * 2**20
        ),
    )(tokens, ids, wts, inv, gate_blocks, up_blocks, down_blocks)


def solution(mesh):
    both = ("dp", "expert")
    return jax.shard_map(
        per_device,
        mesh=mesh,
        in_specs=(
            P(both, "tensor"),
            P(both, None),
            P(both, None),
            P(both, "tensor", None),
            P(both, "tensor", None, None, None),
            P(both, "tensor", None, None, None),
            P(both, "tensor", None, None, None),
        ),
        out_specs=P(both, "tensor"),
        check_vma=False,
    )
```

```python
import functools
import math

import jax
import jax.numpy as jnp
from jax import lax
from jax.experimental import pallas as pl
from jax.experimental.pallas import tpu as pltpu
from jax.sharding import PartitionSpec as P

BLK = 128
PIECES = 8
F32, BF16 = jnp.float32, jnp.bfloat16
MESH = pl.DeviceIdType.MESH


def matmul(a, b):
    return jnp.dot(a, b, preferred_element_type=F32)


def layer_kernel(cfg, tok, ids_ref, wts_ref, topo, gate, up, down, out, *scratch):
    n_dp, n_z, n_x, cap, toks, width, kb, hb = cfg
    (gbuf, ubuf, dbuf, gu, dn, tabs_out, tabs, tokp, zbuf, qa, va, disp, ct, comb_hi, comb_lo, ysend, xin, acc, hid,
     asend, arecv, bsend_r, bsend_l, brecv_l, brecv_r, fsend, yret, gsend, zret,
     w_sem, t_send, t_recv, z_send, z_recv, y_send, y_recv, r1_send, l1_send, r1_recv, l1_recv, r2_send, l2_send,
     r2_recv, l2_recv, ar_send, al_send, ar_recv, al_recv, br_send, bl_send, br_recv, bl_recv,
     f_send, f_recv, g_send, g_recv) = scratch
    pieces = xin.shape[1]
    w = width // pieces
    grp = n_z * cap
    rows = n_dp * grp
    half = rows // 2
    all_tok = n_z * toks
    hid_w = hb * BLK
    per = w // BLK
    dp, z, x = lax.axis_index("dp"), lax.axis_index("expert"), lax.axis_index("tensor")
    right, left, far = lax.rem(x + 1, n_x), lax.rem(x + n_x - 1, n_x), lax.rem(x + 2, n_x)

    def remote(src, dst, ssem, rsem, where):
        return pltpu.make_async_remote_copy(
            src_ref=src, dst_ref=dst, send_sem=ssem, recv_sem=rsem, device_id=where, device_id_type=MESH)

    def drain(ref, sem):
        pltpu.make_async_copy(ref, ref, sem).wait()

    weight_copies = [
        pltpu.make_async_copy(src.at[0], buf.at[:, pl.ds(0, kb)], w_sem.at[i])
        for i, (src, buf) in enumerate(((gate, gbuf), (up, ubuf), (down, dbuf)))
    ]
    for c in weight_copies:
        c.start()

    barrier = pltpu.get_barrier_semaphore()

    def greet_dp(i, _):
        pl.semaphore_signal(barrier, inc=1, device_id={"dp": lax.rem(dp + i, n_dp)}, device_id_type=MESH)
        return 0

    def greet_z(i, _):
        pl.semaphore_signal(barrier, inc=1, device_id={"expert": lax.rem(z + i, n_z)}, device_id_type=MESH)
        return 0

    lax.fori_loop(1, n_dp, greet_dp, 0)
    lax.fori_loop(1, n_z, greet_z, 0)
    pl.semaphore_signal(barrier, inc=1, device_id={"tensor": right}, device_id_type=MESH)
    pl.semaphore_signal(barrier, inc=1, device_id={"tensor": left}, device_id_type=MESH)

    n_e = n_z * n_dp
    q = lax.broadcasted_iota(jnp.int32, (n_e, 2 * toks), 0)
    lane = lax.broadcasted_iota(jnp.int32, (n_e, 2 * toks), 1)
    shift = n_dp.bit_length() - 1
    expert = (q & (n_dp - 1)) * n_z + (q >> shift)
    ids = jnp.concatenate([ids_ref[...], ids_ref[...]], axis=1)
    wts = jnp.concatenate([wts_ref[...], wts_ref[...]], axis=1)
    named = jnp.zeros((n_e, 2 * toks), F32)
    weight = jnp.zeros((n_e, 2 * toks), F32)
    for k in range(ids.shape[0]):
        same = ids[k : k + 1, :] == expert
        named = named + jnp.where(same, 1.0, 0.0)
        weight = weight + jnp.where(same, wts[k : k + 1, :], 0.0)
    before = lax.broadcasted_iota(jnp.int32, (2 * toks, 2 * toks), 0)
    after = lax.broadcasted_iota(jnp.int32, (2 * toks, 2 * toks), 1) & (toks - 1)
    earlier = jnp.where((before < after) & (before < toks), 1.0, 0.0).astype(BF16)
    slot = matmul(named.astype(BF16), earlier)
    table = jnp.where(lane < toks, jnp.where(named > 0.5, slot, -1.0), weight)
    tabs_out[...] = table.reshape(n_z, n_dp, 2 * toks)
    for p in range(pieces):
        tokp[p] = tok[:, p * w : (p + 1) * w]

    pl.semaphore_wait(barrier, (n_dp - 1) + (n_z - 1) + 2)

    def send_table(i, _):
        to = lax.rem(z + i, n_z)
        remote(tabs_out.at[to], tabs.at[z], t_send, t_recv, {"expert": to}).start()
        return 0

    lax.fori_loop(1, n_z, send_table, 0)

    def send_tokens(p):
        def send(i, _):
            to = lax.rem(z + i, n_z)
            remote(tokp.at[p], zbuf.at[p, z], z_send.at[p], z_recv.at[p], {"expert": to}).start()
            return 0

        lax.fori_loop(1, n_z, send, 0)

    send_tokens(0)
    send_tokens(1)
    tabs[z] = tabs_out[z]
    for p in range(pieces):
        zbuf[p, z] = tokp[p]

    for buf in (gbuf, ubuf, dbuf):
        buf[:, kb] = jnp.zeros((hb, BLK, BLK), BF16)
    acc[...] = jnp.zeros(acc.shape, F32)
    drain(tabs.at[pl.ds(0, n_z - 1)], t_recv)
    low = lax.broadcasted_iota(jnp.int32, (n_dp, 2 * toks), 1) < toks
    for j in range(n_z // 2):
        one, two = tabs[2 * j], tabs[2 * j + 1]
        qa[:, j * 2 * toks : (j + 1) * 2 * toks] = jnp.where(low, one, pltpu.roll(two, toks, 1))
        va[:, j * 2 * toks : (j + 1) * 2 * toks] = jnp.where(low, pltpu.roll(one, toks, 1), two)
    r = lax.broadcasted_iota(jnp.int32, (grp, all_tok), 0)
    home = jnp.zeros((grp, all_tok), jnp.int32)
    for j in range(1, n_z):
        home = home + jnp.where(r >= cap * j, 1, 0)
    home_of_token = lax.broadcasted_iota(jnp.int32, (grp, all_tok), 1) >> (toks.bit_length() - 1)
    wanted = jnp.where(home == home_of_token, r - cap * home, -2).astype(F32)

    def one_hot(d, _):
        hit = jnp.broadcast_to(qa[pl.ds(d, 1), :], (grp, all_tok)) == wanted
        at = pl.ds(pl.multiple_of(d * grp, grp), grp)
        disp[at, :] = jnp.where(hit, 1.0, 0.0).astype(BF16)
        ct[at, :] = jnp.where(hit, jnp.broadcast_to(va[pl.ds(d, 1), :], (grp, all_tok)), 0.0)
        return 0

    lax.fori_loop(0, n_dp, one_hot, 0)

    def dense(i, _):
        for j in range(per):
            b = i * per + j
            for h in range(hb):
                at = kb
                for k in range(kb):
                    at = jnp.where(topo[h, 0, k] == b, k, at)
                gu[i, j * BLK : (j + 1) * BLK, h * BLK : (h + 1) * BLK] = gbuf[h, at]
                gu[i, j * BLK : (j + 1) * BLK, hid_w + h * BLK : hid_w + (h + 1) * BLK] = ubuf[h, at]
                dn[i, h * BLK : (h + 1) * BLK, j * BLK : (j + 1) * BLK] = dbuf[h, at]
        return 0


    third = rows // 3

    def gather_piece(p):
        drain(zbuf.at[p, pl.ds(0, n_z - 1)], z_recv.at[p])
        t = zbuf[p].reshape(all_tok, w)

        def tile(i, _):
            at = pl.ds(pl.multiple_of(i * third, 16), third)
            ysend[p, at, :] = matmul(disp[at, :], t).astype(BF16)
            return 0

        lax.fori_loop(0, 3, tile, 0)
        mine = pl.ds(pl.multiple_of(dp * grp, 16), grp)

        def send(i, _):
            to = lax.rem(dp + i, n_dp)
            remote(ysend.at[p, pl.ds(pl.multiple_of(to * grp, 16), grp)], xin.at[x, p, mine],
                   y_send.at[p], y_recv.at[p], {"dp": to}).start()
            return 0

        lax.fori_loop(1, n_dp, send, 0)
        xin[x, p, mine, :] = ysend[p, mine, :]

    def spread_piece(p):
        drain(xin.at[x, p, pl.ds(0, rows - grp)], y_recv.at[p])
        src = xin.at[x, p]
        remote(src, src, r1_send.at[p], r1_recv.at[p], {"tensor": right}).start()
        remote(src, src, l1_send.at[p], l1_recv.at[p], {"tensor": left}).start()

    def forward_piece(p):
        drain(xin.at[left, p], r1_recv.at[p])
        src = xin.at[left, p, pl.ds(0, half)]
        remote(src, src, r2_send.at[p], r2_recv.at[p], {"tensor": right}).start()
        drain(xin.at[right, p], l1_recv.at[p])
        src = xin.at[right, p, pl.ds(half, half)]
        remote(src, src, l2_send.at[p], l2_recv.at[p], {"tensor": left}).start()

    tile = half // 2

    def add_rows(quarters, p, first, tiles):
        def add(i, _):
            at = pl.ds(pl.multiple_of(i * tile, 16), tile)
            acc[at, :] += sum(matmul(xin[k, p, at, :], gu[k * pieces + p]) for k in quarters)
            return 0

        lax.fori_loop(first, first + tiles, add, 0)

    def split_weights():
        tr = math.gcd(rows, BLK)
        for j in range(rows // tr):
            c = ct[j * tr : (j + 1) * tr, :].T
            hi = c.astype(BF16)
            comb_hi[:, j * tr : (j + 1) * tr] = hi
            comb_lo[:, j * tr : (j + 1) * tr] = (c - hi.astype(F32)).astype(BF16)

    def inward(t, _):
        @pl.when(t < pieces)
        def _():
            gather_piece(t)

        @pl.when(t + 2 < pieces)
        def _():
            send_tokens(t + 2)

        @pl.when(t == 0)
        def _():
            for c in weight_copies:
                c.wait()
            lax.fori_loop(0, n_x * pieces, dense, 0)

        @pl.when(t == 1)
        def _():
            split_weights()

        @pl.when((t >= 1) & (t < pieces + 1))
        def _():
            spread_piece(t - 1)

        @pl.when((t >= 2) & (t < pieces + 2))
        def _():
            forward_piece(t - 2)
            add_rows((x, left, right), t - 2, 0, 4)

        @pl.when(t >= 3)
        def _():
            drain(xin.at[far, t - 3, pl.ds(0, half)], r2_recv.at[t - 3])
            drain(xin.at[far, t - 3, pl.ds(half, half)], l2_recv.at[t - 3])
            add_rows((far,), t - 3, 0, 4)

        return 0

    lax.fori_loop(0, pieces + 2, inward, 0)

    def activate(i, _):
        at = pl.ds(pl.multiple_of(i * tile, 16), tile)
        g = acc[at, :hid_w]
        hid[at, :] = (g / (1.0 + jnp.exp(-g)) * acc[at, hid_w:]).astype(BF16)
        return 0

    def partial(quarter, p, part):
        return matmul(hid[part * half : (part + 1) * half, :], dn[quarter * pieces + p])

    lo, hi_ = pl.ds(0, half), pl.ds(half, half)

    def send_far_lo(p):
        asend[p, lo, :] = partial(far, p, 0).astype(BF16)
        remote(asend.at[p, lo], arecv.at[p, lo], ar_send.at[p], ar_recv.at[p], {"tensor": right}).start()

    def send_far_hi(p):
        asend[p, hi_, :] = partial(far, p, 1).astype(BF16)
        remote(asend.at[p, hi_], arecv.at[p, hi_], al_send.at[p], al_recv.at[p], {"tensor": left}).start()

    def send_far(p):
        send_far_lo(p)
        send_far_hi(p)

    def send_near(p):
        bsend_r[p, hi_, :] = partial(right, p, 1).astype(BF16)
        bsend_l[p, lo, :] = partial(left, p, 0).astype(BF16)
        drain(arecv.at[p, lo], ar_recv.at[p])
        bsend_r[p, lo, :] = (partial(right, p, 0) + arecv[p, lo, :].astype(F32)).astype(BF16)
        remote(bsend_r.at[p], brecv_l.at[p], br_send.at[p], br_recv.at[p], {"tensor": right}).start()
        drain(arecv.at[p, hi_], al_recv.at[p])
        bsend_l[p, hi_, :] = (partial(left, p, 1) + arecv[p, hi_, :].astype(F32)).astype(BF16)
        remote(bsend_l.at[p], brecv_r.at[p], bl_send.at[p], bl_recv.at[p], {"tensor": left}).start()

    def send_home(p):
        drain(brecv_l.at[p], br_recv.at[p])
        drain(brecv_r.at[p], bl_recv.at[p])
        for part, at in ((0, lo), (1, hi_)):
            total = partial(x, p, part) + brecv_l[p, at, :].astype(F32) + brecv_r[p, at, :].astype(F32)
            fsend[p, at, :] = total.astype(BF16)
        mine = pl.ds(pl.multiple_of(dp * grp, 16), grp)

        def send(i, _):
            to = lax.rem(dp + i, n_dp)
            remote(fsend.at[p, pl.ds(pl.multiple_of(to * grp, 16), grp)], yret.at[p, mine],
                   f_send.at[p], f_recv.at[p], {"dp": to}).start()
            return 0

        lax.fori_loop(1, n_dp, send, 0)
        yret[p, mine, :] = fsend[p, mine, :]

    def combine(p):
        drain(yret.at[p, pl.ds(0, rows - grp)], f_recv.at[p])

        def tile(i, _):
            at = pl.ds(pl.multiple_of(i * 2 * toks, 2 * toks), 2 * toks)
            s = matmul(comb_hi[at, :], yret[p]) + matmul(comb_lo[at, :], yret[p])
            gsend[p, pl.ds(2 * i, 2)] = s.astype(BF16).reshape(2, toks, w)
            return 0

        lax.fori_loop(0, n_z // 2, tile, 0)

        def send(i, _):
            to = lax.rem(z + i, n_z)
            remote(gsend.at[p, to], zret.at[p, z], g_send.at[p], g_recv.at[p], {"expert": to}).start()
            return 0

        lax.fori_loop(1, n_z, send, 0)
        zret[p, z] = gsend[p, z]

    def finish(p):
        drain(zret.at[p, pl.ds(0, n_z - 1)], g_recv.at[p])
        total = zret[p, 0].astype(F32)
        for h in range(1, n_z):
            total = total + zret[p, h].astype(F32)
        out[:, pl.ds(pl.multiple_of(p * w, BLK), w)] = total.astype(BF16)

    def settle_inward(p):
        drain(zbuf.at[p, pl.ds(0, n_z - 1)], z_send.at[p])
        drain(ysend.at[p, pl.ds(0, rows - grp)], y_send.at[p])
        drain(xin.at[0, p], r1_send.at[p])
        drain(xin.at[0, p], l1_send.at[p])
        drain(xin.at[0, p, lo], r2_send.at[p])
        drain(xin.at[0, p, lo], l2_send.at[p])

    last = pieces - 1
    drain(xin.at[far, last, lo], r2_recv.at[last])
    add_rows((far,), last, 0, 2)
    lax.fori_loop(0, 2, activate, 0)
    send_far_lo(0)
    drain(xin.at[far, last, hi_], l2_recv.at[last])
    add_rows((far,), last, 2, 2)
    lax.fori_loop(2, 4, activate, 0)
    send_far_hi(0)
    send_far(1)
    send_far(2)

    def settle_outward(p):
        drain(asend.at[p, lo], ar_send.at[p])
        drain(asend.at[p, lo], al_send.at[p])
        drain(bsend_r.at[p], br_send.at[p])
        drain(bsend_l.at[p], bl_send.at[p])
        drain(fsend.at[p, pl.ds(0, rows - grp)], f_send.at[p])
        drain(gsend.at[p, pl.ds(0, n_z - 1)], g_send.at[p])

    def outward(t, _):
        @pl.when(t < pieces)
        def _():
            send_near(t)

        @pl.when(t + 3 < pieces)
        def _():
            send_far(t + 3)

        @pl.when((t >= 1) & (t < pieces + 1))
        def _():
            send_home(t - 1)

        @pl.when((t >= 2) & (t < pieces + 2))
        def _():
            combine(t - 2)

        @pl.when(t < pieces)
        def _():
            settle_inward(t)

        @pl.when(t >= 3)
        def _():
            finish(t - 3)
            settle_outward(t - 3)

        return 0

    lax.fori_loop(0, pieces + 3, outward, 0)
    drain(tabs_out.at[pl.ds(0, n_z - 1)], t_send)


def per_device(tokens, expert_ids, combine_weights, topology, gate_blocks, up_blocks, down_blocks):
    n_dp, n_z, n_x = (lax.axis_size(a) for a in ("dp", "expert", "tensor"))
    toks, width = tokens.shape
    top = expert_ids.shape[1]
    cap = min(toks, 3 * toks * top // (2 * n_dp * n_z))
    _, hb, kb = topology.shape
    pieces, w = PIECES, width // PIECES
    rows, grp = n_dp * n_z * cap, n_z * cap
    vm, dma = pltpu.VMEM, pltpu.SemaphoreType.DMA
    hid_w = hb * BLK
    scratch = (
        [vm((hb, kb + 1, BLK, BLK), BF16)] * 3
        + [
            vm((n_x * pieces, w, 2 * hid_w), BF16),
            vm((n_x * pieces, hid_w, w), BF16),
            vm((n_z, n_dp, 2 * toks), F32),
            vm((n_z, n_dp, 2 * toks), F32),
            vm((pieces, toks, w), BF16),
            vm((pieces, n_z, toks, w), BF16),
            vm((n_dp, n_z * toks), F32),
            vm((n_dp, n_z * toks), F32),
            vm((rows, n_z * toks), BF16),
            vm((rows, n_z * toks), F32),
            vm((n_z * toks, rows), BF16),
            vm((n_z * toks, rows), BF16),
            vm((pieces, rows, w), BF16),
            vm((n_x, pieces, rows, w), BF16),
            vm((rows, 2 * hid_w), F32),
            vm((rows, hid_w), BF16),
        ]
        + [vm((pieces, rows, w), BF16)] * 8
        + [vm((pieces, n_z, toks, w), BF16)] * 2
        + [dma((3,)), dma(()), dma(())]
        + [dma((pieces,))] * 24
    )
    any_ = pl.BlockSpec(memory_space=pl.ANY)
    vmem = pl.BlockSpec(memory_space=pltpu.VMEM)
    return pl.pallas_call(
        functools.partial(layer_kernel, (n_dp, n_z, n_x, cap, toks, width, kb, hb)),
        out_shape=jax.ShapeDtypeStruct((toks, width), BF16),
        in_specs=[vmem, vmem, vmem, pl.BlockSpec(memory_space=pltpu.SMEM), any_, any_, any_],
        out_specs=vmem,
        scratch_shapes=scratch,
        compiler_params=pltpu.CompilerParams(
            collective_id=0, has_side_effects=True, vmem_limit_bytes=60 * 2**20
        ),
    )(tokens, expert_ids.T, combine_weights.T, topology.transpose(1, 0, 2), gate_blocks, up_blocks, down_blocks)


def solution(mesh):
    both = ("dp", "expert")
    return jax.shard_map(
        per_device,
        mesh=mesh,
        in_specs=(
            P(both, "tensor"),
            P(both, None),
            P(both, None),
            P(both, "tensor", None),
            P(both, "tensor", None, None, None),
            P(both, "tensor", None, None, None),
            P(both, "tensor", None, None, None),
        ),
        out_specs=P(both, "tensor"),
        check_vma=False,
    )
```
